32 devices in a mesh: tp: 2 (over x), dp: 16 (over z, y, core).
Axes of the slice: x: 2, y: 2, z: 4, core: 2. Of those that a mesh axis runs over, the one named last changes fastest.
Arguments:
- residual: bfloat16 [768, 8192], P('tp', 'dp'), may hold values from -6 to 6
- queries: bfloat16 [768, 8192], P('dp', 'tp'), may hold values from -33 to 33
- new_kv: bfloat16 [768, 2048], P('dp', 'tp'), may hold values from -6.05 to 6.05
- cache: bfloat16 [16, 2048, 2048], P('dp', None, 'tp'), may hold values from -6 to 6
- cache_len: int32 [16], P('dp'), may hold values from 1 to 2048, 16384 in all
- tree_parent: int32 [16, 48], P('dp'), may hold values from -1 to 36, as said below
- accepted_tip: int32 [16], replicated, may hold values from 0 to 47
- slot_request: int32 [16], replicated, may hold values from 0 to 15, each once
- out_weight: bfloat16 [8192, 8192], P('tp', 'dp'), may hold values from -0.25 to 0.25
- final_gain: bfloat16 [8192], replicated, may hold values from 0.25 to 1.75
- medusa_up: bfloat16 [4, 8192, 8192], P(None, 'dp', 'tp'), may hold values from -0.0625 to 0.0625
- medusa_vocab: bfloat16 [4, 8192, 16384], P(None, 'tp', 'dp'), may hold values from -0.0625 to 0.0625
Outputs:
- hidden_out: bfloat16 [768, 8192], P('tp', 'dp')
- medusa_logits: bfloat16 [4, 16, 16384], P(None, 'tp', 'dp')
- accepted_kv: bfloat16 [16, 5, 2048], P('dp', None, 'tp')
The draws below stay inside these ranges and needn't reach their ends.
Inputs may be any that keep to these rules, and one draw needn't show every extreme that they name: tree_parent[j, 0] = -1; for a node i >= 1 the parent is an earlier node, and no node lies more than 4 steps below node 0; node 47 lies exactly 4 steps below it, and its parent is the last node of the level above it. `cache_len`: the longest cache holds exactly 2048 positions.
All inputs are finite; a program needn't handle non-finite values. No bound on the sum of `cache_len` on one device may be relied on, other than what follows from the above.
Results may differ from the reference program's by a relative error of at most 0.0069.
Values may be sent and summed in bfloat16 or wider, within the bound.
A program may use at most 192 MiB of HBM per device.

```python
import math
import jax
import jax.numpy as jnp
import numpy as np
from jax import lax

D = 8192
HQ = 64
HK = 8
HD = 128
VOC = 16384
MED = 4
TREE = 48
DEPTH = 5
CMAX = 2048
REQS = 16
TOK = 768


def tree_parents(key):
    nodes = jnp.arange(TREE, dtype=jnp.int32)
    depth_of = jnp.where(nodes == 0, 0, 1 + (nodes - 1) * (DEPTH - 1) // (TREE - 1))

    def level_start(level_value):
        return jnp.where(level_value <= 0, 0, 1 + ((level_value - 1) * (TREE - 1) + DEPTH - 2) // (DEPTH - 1))
    lower_bound = level_start(depth_of - 1).astype(jnp.int32)
    upper_bound = jnp.maximum(level_start(depth_of), lower_bound + 1).astype(jnp.int32)
    drawn = jax.random.randint(jax.random.fold_in(key, 11), (REQS, TREE), lower_bound[None, :], upper_bound[None, :], dtype=jnp.int32)
    drawn = jnp.where(nodes[None, :] == TREE - 1, upper_bound[None, :] - 1, drawn)
    return jnp.where(nodes[None, :] == 0, -1, drawn).astype(jnp.int32)


def fresh_base(key):
    return jnp.clip(jax.random.normal(jax.random.fold_in(key, 22), (REQS, TREE, HK, 2, HD), jnp.float32), -6.0, 6.0)


def draw_new_kv(key, part):
    fresh = fresh_base(key)
    return fresh.reshape(TOK, HK * 2 * HD).astype(jnp.bfloat16)


def draw_queries(key, part):
    parents = tree_parents(key)
    fresh = fresh_base(key)
    keys_only = fresh[:, :, :, 0, :]
    current = jnp.broadcast_to(jnp.arange(TREE, dtype=jnp.int32)[None, :], (REQS, TREE))
    summed_keys = keys_only
    for repeat_index in range(DEPTH - 1):
        current = jnp.where(current >= 0, jnp.take_along_axis(parents, jnp.maximum(current, 0), axis=1), -1)
        picked = jnp.take_along_axis(keys_only, jnp.maximum(current, 0)[:, :, None, None], axis=1)
        summed_keys = summed_keys + jnp.where((current >= 0)[:, :, None, None], picked, 0.0)
    noise = jnp.clip(jax.random.normal(jax.random.fold_in(key, 23), (REQS, TREE, HK, HQ // HK, HD), jnp.float32), -6.0, 6.0)
    result = 0.5 * summed_keys[:, :, :, None, :] + noise
    return result.reshape(TOK, HQ * HD).astype(jnp.bfloat16)


def draw_cache(key, part):
    stored = jnp.clip(jax.random.normal(jax.random.fold_in(key, 24), (REQS, CMAX, HK, 2, HD), jnp.float32), -6.0, 6.0)
    return stored.reshape(REQS, CMAX, HK * 2 * HD).astype(jnp.bfloat16)


def draw_tree_parent(key, part):
    return tree_parents(key)


def draw_accepted_tip(key, part):
    drawn = jax.random.randint(jax.random.fold_in(key, 31), (REQS,), 0, TREE, dtype=jnp.int32)
    return jnp.where(jnp.arange(REQS, dtype=jnp.int32) == 0, TREE - 1, drawn).astype(jnp.int32)


def block_levels(own_key, extent, shards, smallest, top_value):
    factor_of = 1.0
    for dim, shards_of in shards:
        steps = jax.random.uniform(jax.random.fold_in(jax.random.fold_in(own_key, 6), dim), (shards_of,), jnp.float32, smallest / len(shards), top_value / len(shards))
        factor_of = factor_of * jnp.repeat(jnp.exp(steps), extent[dim] // shards_of).reshape((-1,) + (1,) * (len(extent) - 1 - dim))
    return factor_of


def profile(amount, total, limit, lean):
    loads = [(1 << 20) // math.isqrt(rank ** lean) + 1 for rank in range(2, amount + 1)]
    surplus, counts = total - limit - (amount - 1), [1] * (amount - 1)
    while surplus > 0:
        movable = [i for i in range(amount - 1) if counts[i] < limit]
        whole, budget = sum([loads[i] for i in movable]), surplus
        for i in movable:
            extra = min(limit - counts[i], max(1, budget * loads[i] // whole), surplus)
            counts[i] = counts[i] + extra
            surplus = surplus - extra
    return np.array([limit] + counts)


def uneven_parts(rng, number_of, total, reach, skew):
    if number_of == 2:
        one = jax.random.randint(rng, (), max(1, total - reach), min(reach, total - 1) + 1)
        return jnp.stack([one, total - one])
    lengths = jnp.asarray(profile(number_of, total, reach, skew), jnp.int32)
    pairs = (number_of - 1) // 2
    donor, taker = lengths[1:1 + 2 * pairs:2], lengths[2:2 + 2 * pairs:2]
    room = jnp.minimum(donor - 1, reach - taker)
    shifted = jax.random.randint(jax.random.fold_in(rng, 1), (pairs,), 0, 1 << 20) % (room + 1)
    lengths = lengths.at[1:1 + 2 * pairs:2].set(donor - shifted).at[2:2 + 2 * pairs:2].set(taker + shifted)
    return lengths[jax.random.permutation(jax.random.fold_in(rng, 2), number_of)]


def centred(key, shape, width, bound, shards=(), kind=jnp.bfloat16):
    entries = jax.random.normal(key, shape, jnp.float32) * width
    if len(shards) > 0:
        entries = block_levels(key, shape, shards, -0.22, 0.18) * entries
    return jnp.clip(entries, min=-bound, max=bound).astype(kind)


def setup_inputs(seed: int = 0) -> dict:
    key_of = jax.random.split(jax.random.key(seed), 13)
    residual = centred(key_of[0], (TOK, D), 1.0, 6.0, ((0, 2), (1, 16)))
    queries = draw_queries(jax.random.fold_in(key_of[12], 71), 0)
    new_kv = draw_new_kv(jax.random.fold_in(key_of[12], 71), 0)
    cache = draw_cache(jax.random.fold_in(key_of[12], 71), 0)
    cache_len = uneven_parts(key_of[4], REQS, REQS * CMAX // 2, CMAX, 2).astype(jnp.int32)
    tree_parent = draw_tree_parent(jax.random.fold_in(key_of[12], 71), 0)
    accepted_tip = draw_accepted_tip(jax.random.fold_in(key_of[12], 71), 0)
    slot_request = jax.random.permutation(key_of[7], REQS).astype(jnp.int32)
    out_weight = centred(key_of[8], (HQ * HD, D), (HQ * HD // 16) ** -0.5, 0.25, ((0, 2), (1, 16)))
    final_gain = jnp.clip(1.0 + 0.15 * jax.random.normal(key_of[9], (D,), jnp.float32), 0.25, 1.75).astype(jnp.bfloat16)
    medusa_up = centred(key_of[10], (MED, D, D), D ** -0.5, 0.0625, ((1, 16), (2, 2)))
    medusa_vocab = centred(key_of[11], (MED, D, VOC), D ** -0.5, 0.0625, ((1, 2), (2, 16)))
    return {"residual": residual, "queries": queries, "new_kv": new_kv, "cache": cache, "cache_len": cache_len, "tree_parent": tree_parent, "accepted_tip": accepted_tip, "slot_request": slot_request, "out_weight": out_weight, "final_gain": final_gain, "medusa_up": medusa_up, "medusa_vocab": medusa_vocab}


NEG = -1e+30

def climb_tree(parent_row, start_nodes):
    chain = [start_nodes]
    current = start_nodes
    for repeat_index in range(DEPTH - 1):
        current = jnp.where(current >= 0, parent_row[jnp.maximum(current, 0)], -1).astype(jnp.int32)
        chain.append(current)
    return jnp.stack(chain)

def ancestry_mask(parent_row):
    nodes = jnp.arange(TREE, dtype=jnp.int32)
    upward = climb_tree(parent_row, nodes)
    return jnp.any(upward[:, :, None] == nodes[None, None, :], axis=0)

def attend_slot(operands):
    query_rows, fresh_rows, cache_rows, live_length, parent_row = operands
    query_heads = query_rows.reshape(TREE, HK, HQ // HK, HD).astype(jnp.float32)
    fresh = fresh_rows.reshape(TREE, HK, 2, HD).astype(jnp.float32)
    stored = cache_rows.reshape(CMAX, HK, 2, HD).astype(jnp.float32)
    scale_factor = 1.0 / math.sqrt(HD)
    cache_scores = jnp.einsum('igrd,pgd->igrp', query_heads, stored[:, :, 0]) * scale_factor
    tree_scores = jnp.einsum('igrd,mgd->igrm', query_heads, fresh[:, :, 0]) * scale_factor
    positions = jnp.arange(CMAX, dtype=jnp.int32)
    cache_scores = jnp.where(positions[None, None, None, :] < live_length, cache_scores, NEG)
    allowed = ancestry_mask(parent_row)
    tree_scores = jnp.where(allowed[:, None, None, :], tree_scores, NEG)
    scores = jnp.concatenate([cache_scores, tree_scores], axis=-1)
    highest = lax.optimization_barrier(jnp.max(scores, axis=-1, keepdims=True))
    weights_full = jnp.exp(scores - highest)
    totals = lax.optimization_barrier(jnp.sum(weights_full, axis=-1, keepdims=True))
    weights_low = lax.optimization_barrier(weights_full.astype(jnp.bfloat16)).astype(jnp.float32)
    values_all = jnp.concatenate([stored[:, :, 1], fresh[:, :, 1]], axis=0)
    mixed = jnp.einsum('igrp,pgd->igrd', weights_low, values_all) / totals
    return mixed.astype(jnp.bfloat16).reshape(TREE, HQ * HD)

def compact_path(parent_row, tip_node, fresh_rows):
    upward = climb_tree(parent_row, tip_node)
    path_length = jnp.sum((upward >= 0).astype(jnp.int32))
    order = path_length - 1 - jnp.arange(DEPTH, dtype=jnp.int32)
    picked = upward[jnp.maximum(order, 0)]
    chosen_rows = fresh_rows[picked]
    return jnp.where((order >= 0)[:, None], chosen_rows, jnp.zeros_like(chosen_rows))

def reference(residual, queries, new_kv, cache, cache_len, tree_parent, accepted_tip, slot_request, out_weight, final_gain, medusa_up, medusa_vocab):
    attended = lax.map(attend_slot, (queries.reshape(REQS, TREE, HQ * HD), new_kv.reshape(REQS, TREE, HK * 2 * HD), cache, cache_len, tree_parent))
    attended = attended.reshape(TOK, HQ * HD)
    projected = jnp.dot(attended, out_weight, preferred_element_type=jnp.float32)
    slot_of = jnp.zeros((REQS,), jnp.int32).at[slot_request].set(jnp.arange(REQS, dtype=jnp.int32))
    projected = projected.reshape(REQS, TREE, D)[slot_of].reshape(TOK, D)
    hidden_out = (residual.astype(jnp.float32) + projected).astype(jnp.bfloat16)
    tip_hidden = hidden_out.reshape(REQS, TREE, D)[jnp.arange(REQS), accepted_tip].astype(jnp.float32)
    mean_square = lax.optimization_barrier(jnp.mean(tip_hidden * tip_hidden, axis=-1, keepdims=True))
    normed = (tip_hidden * lax.rsqrt(mean_square + 1e-05) * final_gain.astype(jnp.float32)).astype(jnp.bfloat16)
    logits_list = []
    for head_index in range(MED):
        lifted = jnp.dot(normed, medusa_up[head_index], preferred_element_type=jnp.float32)
        drafted = (normed.astype(jnp.float32) + jax.nn.silu(lifted)).astype(jnp.bfloat16)
        logits_list.append(jnp.dot(drafted, medusa_vocab[head_index], preferred_element_type=jnp.float32).astype(jnp.bfloat16))
    medusa_logits = jnp.stack(logits_list)
    tips_by_slot = accepted_tip[slot_request]
    accepted_kv = jax.vmap(compact_path)(tree_parent, tips_by_slot, new_kv.reshape(REQS, TREE, HK * 2 * HD))
    return (hidden_out, medusa_logits, accepted_kv)
```

```python
import functools
import math

import jax
import jax.numpy as jnp
from jax import lax
from jax.experimental import pallas as pl
from jax.experimental.pallas import tpu as pltpu
from jax.sharding import PartitionSpec as P

HD = 128
TREE = 48
DEPTH = 5
NEG = -1e30
F32 = jnp.float32
BF16 = jnp.bfloat16
MIB = 1 << 20


def dot(a, b):
    return jnp.dot(a, b, preferred_element_type=F32)


def attend_kernel(len_ref, tip_ref, par_smem, par_ref, q_ref, new_ref, cache_ref, att_ref, row_ref, acc_ref):
    group = q_ref.shape[1] // HD
    rows = group * TREE
    length = cache_ref.shape[1]
    scale = 1.0 / math.sqrt(HD)
    live = len_ref[0]
    tip = tip_ref[0]

    nodes = lax.broadcasted_iota(jnp.int32, (TREE, TREE), 1)
    own = lax.broadcasted_iota(jnp.int32, (TREE, TREE), 0)
    step = (par_ref[...] == nodes).astype(F32).astype(BF16)
    reach = (own == nodes).astype(F32)
    total_reach = reach
    for _ in range(DEPTH - 1):
        reach = dot(reach.astype(BF16), step)
        total_reach = total_reach + reach
    allowed = jnp.concatenate([total_reach] * group, axis=0) > 0.5

    q = jnp.concatenate([q_ref[:, r * HD:(r + 1) * HD] for r in range(group)], axis=0)
    keys = cache_ref[0, :, :HD]
    values = cache_ref[0, :, HD:]
    new_keys = new_ref[:, :HD]
    new_values = new_ref[:, HD:]
    contract = (((1,), (1,)), ((), ()))
    scores = lax.dot_general(q, keys, contract, preferred_element_type=F32) * scale
    place = lax.broadcasted_iota(jnp.int32, (1, length), 1)
    scores = jnp.where(place < live, scores, NEG)
    fresh = lax.dot_general(q, new_keys, contract, preferred_element_type=F32) * scale
    fresh = jnp.where(allowed, fresh, NEG)
    high = jnp.maximum(jnp.max(scores, axis=1, keepdims=True), jnp.max(fresh, axis=1, keepdims=True))
    weights = jnp.exp(scores - high)
    fresh_weights = jnp.exp(fresh - high)
    total = jnp.sum(weights, axis=1, keepdims=True) + jnp.sum(fresh_weights, axis=1, keepdims=True)
    mixed = dot(weights.astype(BF16), values) + dot(fresh_weights.astype(BF16), new_values)
    attended = (mixed / total).astype(BF16)
    for r in range(group):
        att_ref[:, r * HD:(r + 1) * HD] = attended[r * TREE:(r + 1) * TREE]
    lane = lax.broadcasted_iota(jnp.int32, (group, rows), 1)
    want = lax.broadcasted_iota(jnp.int32, (group, rows), 0) * TREE + tip
    row_ref[...] = dot((lane == want).astype(F32).astype(BF16), attended).astype(row_ref.dtype)

    chain = [tip]
    for _ in range(DEPTH - 1):
        last = chain[-1]
        chain.append(jnp.where(last >= 0, par_smem[0, jnp.maximum(last, 0)], -1))
    count = sum((c >= 0).astype(jnp.int32) for c in chain)
    slot = lax.broadcasted_iota(jnp.int32, (16, TREE), 0)
    node = lax.broadcasted_iota(jnp.int32, (16, TREE), 1)
    pick = jnp.zeros((16, TREE), F32)
    for k in range(DEPTH):
        hit = (slot == count - 1 - k) & (node == chain[k])
        pick = pick + hit.astype(F32)
    picked = dot(pick.astype(BF16), new_ref[...])
    acc_ref[0] = picked[:DEPTH].astype(BF16)


def attend(queries, new_kv, cache, cache_len, tree_parent, tip, row_dtype):
    heads = cache.shape[2] // (2 * HD)
    group = queries.shape[1] // (heads * HD)
    length = cache.shape[1]
    smem = pl.BlockSpec(memory_space=pltpu.SMEM)
    return pl.pallas_call(
        attend_kernel,
        grid=(heads,),
        in_specs=[
            smem,
            smem,
            smem,
            pl.BlockSpec((TREE, 1), lambda g: (0, 0)),
            pl.BlockSpec((TREE, group * HD), lambda g: (0, g)),
            pl.BlockSpec((TREE, 2 * HD), lambda g: (0, g)),
            pl.BlockSpec((1, length, 2 * HD), lambda g: (0, 0, g)),
        ],
        out_specs=[
            pl.BlockSpec((TREE, group * HD), lambda g: (0, g)),
            pl.BlockSpec((group, HD), lambda g: (g, 0)),
            pl.BlockSpec((1, DEPTH, 2 * HD), lambda g: (0, 0, g)),
        ],
        out_shape=[
            jax.ShapeDtypeStruct((TREE, heads * group * HD), BF16),
            jax.ShapeDtypeStruct((heads * group, HD), row_dtype),
            jax.ShapeDtypeStruct((1, DEPTH, heads * 2 * HD), BF16),
        ],
        compiler_params=pltpu.CompilerParams(vmem_limit_bytes=40 * MIB),
    )(cache_len, tip, tree_parent, tree_parent.reshape(TREE, 1), queries, new_kv, cache)


def remote(src, dst, send, recv, **where):
    return pltpu.make_async_remote_copy(
        src_ref=src,
        dst_ref=dst,
        send_sem=send,
        recv_sem=recv,
        device_id=where,
        device_id_type=pl.DeviceIdType.MESH,
    )


class Gather:
    def __init__(self, buf, send, recv, me, outer, mid):
        self.buf, self.send, self.recv = buf, send, recv
        self.outer, self.mid, self.me = outer, mid, me
        self.c = me % 2
        self.m = (me // 2) % mid
        self.o = me // (2 * mid)
        self.started = []

    def at(self, o, m, c):
        return (o * self.mid + m) * 2 + c

    def push(self, block, peer):
        copy = remote(
            self.buf.at[block],
            self.buf.at[block],
            self.send.at[len(self.started)],
            self.recv.at[block],
            dp=peer,
        )
        copy.start()
        self.started.append(copy)

    def arrived(self, block):
        remote(self.buf.at[block], self.buf.at[block], self.send.at[0], self.recv.at[block], dp=self.me).wait_recv()

    def mids(self):
        return [(self.m + d) % self.mid for d in range(1, self.mid)]

    def begin(self):
        for m in self.mids():
            self.push(self.me, self.at(self.o, m, self.c))
        for d in range(1, self.outer):
            self.push(self.me, self.at((self.o + d) % self.outer, self.m, self.c))
        self.push(self.me, self.at(self.o, self.m, 1 - self.c))

    def forward_outer(self, d):
        block = self.at((self.o + d) % self.outer, self.m, self.c)
        self.arrived(block)
        for m in self.mids():
            self.push(block, self.at(self.o, m, self.c))
        self.push(block, self.at(self.o, self.m, 1 - self.c))

    def forward_mid(self):
        for d in range(self.outer):
            for m in self.mids():
                block = self.at((self.o + d) % self.outer, m, self.c)
                self.arrived(block)
                self.push(block, self.at(self.o, self.m, 1 - self.c))

    def finish(self):
        for o in range(self.outer):
            for m in range(self.mid):
                self.arrived(self.at(o, m, 1 - self.c))

    def drain(self):
        for copy in self.started:
            copy.wait_send()


def main_kernel(
    tp, dp, outer, mid,
    slot_of, tips_ref, smat_ref, resid_tip, gain_ref, att_hbm, w_hbm, up_hbm, voc_hbm, resid_hbm,
    hid_out, log_out,
    tipg, w_buf, up_buf, voc_buf, gath, proj, psend, precv, resid_buf,
    xsend, xrecv, hid, part, rec1, acc1, rec2, acc2, rec3, drf, lpart, lrecv,
    w_sem, up_sem, voc_sem, in_sem,
    tip_s, tip_r, x_s, x_r, hid_s, hid_r, c_s, c_r, m_s, m_r, o_s, o_r,
    drf_s, drf_r, bulk_s, bulk_r, l_s, l_r, p_s, p_r,
):
    me = lax.axis_index("dp")
    mt = lax.axis_index("tp")
    c = me % 2
    m = (me // 2) % mid
    o = me // (2 * mid)
    reqs = hid.shape[1]
    heads = up_buf.shape[0]
    width = up_buf.shape[2]
    nq = tips_ref.shape[0]
    colw = hid.shape[2]
    chunk = part.shape[-1]
    row_groups = reqs // 16
    slots = voc_buf.shape[0]
    own_reqs = reqs // tp

    w_copy = pltpu.make_async_copy(w_hbm, w_buf, w_sem)
    w_copy.start()
    own_copy = pltpu.make_async_copy(att_hbm, gath.at[me], in_sem.at[0])
    own_copy.start()
    up_copies = [pltpu.make_async_copy(up_hbm.at[k], up_buf.at[k], up_sem.at[k]) for k in range(heads)]
    voc_copies = [
        pltpu.make_async_copy(voc_hbm.at[k], voc_buf.at[k % slots], voc_sem.at[k]) for k in range(heads)
    ]
    resid_copy = pltpu.make_async_copy(resid_hbm, resid_buf, in_sem.at[1])
    for copy in up_copies:
        copy.start()
    for copy in voc_copies[:slots]:
        copy.start()
    resid_copy.start()

    barrier = pltpu.get_barrier_semaphore()
    for d in range(1, dp):
        pl.semaphore_signal(barrier, inc=1, device_id={"dp": (me + d) % dp}, device_id_type=pl.DeviceIdType.MESH)
    for d in range(1, tp):
        pl.semaphore_signal(barrier, inc=1, device_id={"tp": (mt + d) % tp}, device_id_type=pl.DeviceIdType.MESH)
    pl.semaphore_wait(barrier, dp + tp - 2)

    mine = pl.ds(pl.multiple_of(me * nq, nq), nq)
    tip_copies = []
    for d in range(1, dp):
        copy = remote(tips_ref, tipg.at[mine], tip_s.at[d], tip_r.at[me], dp=(me + d) % dp)
        copy.start()
        tip_copies.append(copy)
    tipg[mine] = tips_ref[...]
    bulk = Gather(gath, bulk_s, bulk_r, me, outer, mid)
    own_copy.wait()
    bulk.begin()
    for d in range(1, dp):
        src = (me + d) % dp
        there = pl.ds(pl.multiple_of(src * nq, nq), nq)
        remote(tips_ref, tipg.at[there], tip_s.at[0], tip_r.at[src], dp=me).wait_recv()
    picked = dot(smat_ref[...], tipg[...].astype(BF16)).astype(BF16)
    tip_rows = jnp.concatenate([picked[i * reqs:(i + 1) * reqs] for i in range(nq)], axis=1)
    w_copy.wait()
    xsend[...] = dot(tip_rows, w_buf[...]) + resid_tip[...]
    x_copies = []
    for d in range(1, tp):
        copy = remote(xsend, xrecv.at[mt], x_s.at[d], x_r.at[mt], tp=(mt + d) % tp)
        copy.start()
        x_copies.append(copy)
    xrecv[mt] = xsend[...]
    for d in range(1, tp):
        src = (mt + d) % tp
        remote(xsend, xrecv.at[src], x_s.at[0], x_r.at[src], tp=mt).wait_recv()
    summed = xrecv[0]
    for d in range(1, tp):
        summed = summed + xrecv[d]
    hid[me] = summed.astype(BF16)
    hid_copies = []
    for d in range(1, dp):
        copy = remote(hid.at[me], hid.at[me], hid_s.at[d], hid_r.at[me], dp=(me + d) % dp)
        copy.start()
        hid_copies.append(copy)
    for d in range(1, dp):
        src = (me + d) % dp
        remote(hid.at[src], hid.at[src], hid_s.at[0], hid_r.at[src], dp=me).wait_recv()
    squares = jnp.zeros((reqs, colw), F32)
    for d in range(dp):
        block = hid[d].astype(F32)
        squares = squares + block * block
    inverse = lax.rsqrt(jnp.sum(squares, axis=1, keepdims=True) * (1.0 / (dp * colw)) + 1e-05)
    normed = (hid[me].astype(F32) * inverse * gain_ref[me]).astype(BF16)

    for k in range(heads):
        up_copies[k].wait()

    def up_head(k, carry):
        for cg in range(4):
            out = dot(normed, up_buf[k, :, cg * chunk:(cg + 1) * chunk]).astype(BF16)
            for rg in range(row_groups):
                e = (k * row_groups + rg) * 4 + cg
                part[e // 2, cg % 2] = out[rg * 16:(rg + 1) * 16]
        return carry

    lax.fori_loop(0, heads, up_head, 0)

    c_copy = remote(part.at[:, 1 - c], rec1, c_s, c_r, dp=(o * mid + m) * 2 + 1 - c)
    c_copy.start()
    c_copy.wait_recv()
    half = part[:, c].astype(F32) + rec1[...].astype(F32)
    acc1[...] = half.astype(BF16).reshape(acc1.shape)
    m_copies = []
    for d in range(1, mid):
        pm = (m + d) % mid
        copy = remote(acc1.at[:, pm], rec2.at[m], m_s.at[d], m_r.at[m], dp=(o * mid + pm) * 2 + c)
        copy.start()
        m_copies.append(copy)
    quarter = acc1[:, m].astype(F32)
    for d in range(1, mid):
        pm = (m + d) % mid
        remote(rec2.at[pm], rec2.at[pm], m_s.at[0], m_r.at[pm], dp=me).wait_recv()
        quarter = quarter + rec2[pm].astype(F32)
    acc2[...] = quarter.astype(BF16)
    o_copies = []
    for d in range(1, outer):
        po = (o + d) % outer
        copy = remote(acc2.at[po], rec3.at[o], o_s.at[d], o_r.at[o], dp=(po * mid + m) * 2 + c)
        copy.start()
        o_copies.append(copy)
    lifted = acc2[o].astype(F32)
    for d in range(1, outer):
        po = (o + d) % outer
        remote(rec3.at[po], rec3.at[po], o_s.at[0], o_r.at[po], dp=me).wait_recv()
        lifted = lifted + rec3[po].astype(F32)
    my_cg = me % 4
    my_rg = (me // 4) % row_groups
    per = chunk // colw
    first = mt * (width // colw) + my_cg * per
    rows16 = pl.ds(pl.multiple_of(my_rg * 16, 16), 16)
    square16 = jnp.zeros((16, colw), F32)
    for d in range(dp):
        block = hid[d, rows16].astype(F32)
        square16 = square16 + block * block
    inverse16 = lax.rsqrt(jnp.sum(square16, axis=1, keepdims=True) * (1.0 / (dp * colw)) + 1e-05)
    skip = jnp.concatenate(
        [
            (hid[first + b, rows16].astype(F32) * inverse16 * gain_ref[first + b]).astype(BF16)
            for b in range(per)
        ],
        axis=1,
    )
    drf[me] = (skip.astype(F32) + lifted / (1.0 + jnp.exp(-lifted))).astype(BF16)
    small = Gather(drf, drf_s, drf_r, me, outer, mid)
    small.begin()
    for d in range(1, outer):
        small.forward_outer(d)
    small.forward_mid()
    small.finish()

    for d in range(1, outer):
        bulk.forward_outer(d)

    l_copies = []
    for k in range(heads):
        voc_copies[k].wait()
        total = None
        for cg in range(4):
            lhs = jnp.concatenate([drf[(k * row_groups + rg) * 4 + cg] for rg in range(row_groups)], axis=0)
            term = dot(lhs, voc_buf[k % slots, cg * chunk:(cg + 1) * chunk, :])
            total = term if total is None else total + term
        lpart[k] = total.reshape(lpart.shape[1:])
        if k + slots < heads:
            voc_copies[k + slots].start()
        for d in range(1, tp):
            pt = (mt + d) % tp
            copy = remote(lpart.at[k, pt], lrecv.at[mt, k], l_s.at[k, d], l_r.at[k, mt], tp=pt)
            copy.start()
            l_copies.append(copy)

    bulk.forward_mid()
    bulk.finish()

    groups = gath.shape[0] // 4

    def project(g, carry):
        block = gath[pl.ds(g * 4, 4)].reshape(4 * TREE, width)
        proj[pl.ds(g * 4, 4)] = dot(block, w_buf[...]).reshape(4, TREE, colw)
        return carry

    lax.fori_loop(0, groups, project, 0)
    p_copies = []
    for d in range(1, tp):
        pt = (mt + d) % tp

        def fill(i, carry, pt=pt, d=d):
            psend[d - 1, i] = proj[slot_of[pt * own_reqs + i]].astype(BF16)
            return carry

        lax.fori_loop(0, own_reqs, fill, 0)
        copy = remote(psend.at[d - 1], precv.at[mt], p_s.at[d], p_r.at[mt], tp=pt)
        copy.start()
        p_copies.append(copy)

    for k in range(heads):
        for d in range(1, tp):
            src = (mt + d) % tp
            remote(lrecv.at[src, k], lrecv.at[src, k], l_s.at[0, 0], l_r.at[k, src], tp=mt).wait_recv()
    for k in range(heads):
        value = lpart[k, mt]
        for d in range(1, tp):
            value = value + lrecv[(mt + d) % tp, k]
        log_out[k] = value.astype(BF16)

    resid_copy.wait()
    for d in range(1, tp):
        src = (mt + d) % tp
        remote(precv.at[src], precv.at[src], p_s.at[0], p_r.at[src], tp=mt).wait_recv()

    def finish(i, carry):
        value = resid_buf[i].astype(F32) + proj[slot_of[mt * own_reqs + i]]
        for d in range(1, tp):
            value = value + precv[(mt + d) % tp, i].astype(F32)
        hid_out[i] = value.astype(BF16)
        return carry

    lax.fori_loop(0, own_reqs, finish, 0)

    for copy in tip_copies + x_copies + hid_copies + [c_copy] + m_copies + o_copies + l_copies + p_copies:
        copy.wait_send()
    small.drain()
    bulk.drain()


def run_main(tp, dp, slot_of, tips, smat, resid_tip, gain, attended, out_weight, up, vocab, residual):
    mid = 2 if dp <= 16 else 4
    outer = dp // (2 * mid)
    heads, colw, width = up.shape
    vcols = vocab.shape[2]
    reqs = resid_tip.shape[0]
    own = reqs // tp
    nq = tips.shape[0]
    chunk = heads * (reqs // 16) * width // dp
    slots = heads - 1
    vmem = pl.BlockSpec(memory_space=pltpu.VMEM)
    hbm = pl.BlockSpec(memory_space=pl.ANY)
    dma = pltpu.SemaphoreType.DMA
    return pl.pallas_call(
        functools.partial(main_kernel, tp, dp, outer, mid),
        in_specs=[pl.BlockSpec(memory_space=pltpu.SMEM), vmem, vmem, vmem, vmem, hbm, hbm, hbm, hbm, hbm],
        out_specs=[vmem, vmem],
        out_shape=[
            jax.ShapeDtypeStruct((own, TREE, colw), BF16),
            jax.ShapeDtypeStruct((heads, own, vcols), BF16),
        ],
        scratch_shapes=[
            pltpu.VMEM((dp * nq, HD), tips.dtype),
            pltpu.VMEM((width, colw), BF16),
            pltpu.VMEM((heads, colw, width), BF16),
            pltpu.VMEM((slots, width, vcols), BF16),
            pltpu.VMEM((dp, TREE, width), BF16),
            pltpu.VMEM((dp, TREE, colw), F32),
            pltpu.VMEM((tp - 1, own, TREE, colw), BF16),
            pltpu.VMEM((tp, own, TREE, colw), BF16),
            pltpu.VMEM((own, TREE, colw), BF16),
            pltpu.VMEM((reqs, colw), F32),
            pltpu.VMEM((tp, reqs, colw), F32),
            pltpu.VMEM((dp, reqs, colw), BF16),
            pltpu.VMEM((dp // 2, 2, 16, chunk), BF16),
            pltpu.VMEM((dp // 2, 16, chunk), BF16),
            pltpu.VMEM((outer, mid, 16, chunk), BF16),
            pltpu.VMEM((mid, outer, 16, chunk), BF16),
            pltpu.VMEM((outer, 16, chunk), BF16),
            pltpu.VMEM((outer, 16, chunk), BF16),
            pltpu.VMEM((dp, 16, chunk), BF16),
            pltpu.VMEM((heads, tp, own, vcols), F32),
            pltpu.VMEM((tp, heads, own, vcols), F32),
            dma(()), dma((heads,)), dma((heads,)), dma((2,)),
            dma((dp,)), dma((dp,)), dma((tp,)), dma((tp,)), dma((dp,)), dma((dp,)),
            dma(()), dma(()), dma((mid,)), dma((mid,)), dma((outer,)), dma((outer,)),
            dma((dp,)), dma((dp,)), dma((dp,)), dma((dp,)),
            dma((heads, tp)), dma((heads, tp)), dma((tp,)), dma((tp,)),
        ],
        compiler_params=pltpu.CompilerParams(
            collective_id=0, has_side_effects=True, vmem_limit_bytes=60 * MIB
        ),
    )(slot_of, tips, smat, resid_tip, gain, attended, out_weight, up, vocab, residual)


def on_device(
    tp, dp,
    residual, queries, new_kv, cache, cache_len, tree_parent, accepted_tip, slot_request,
    out_weight, final_gain, medusa_up, medusa_vocab,
):
    reqs = slot_request.shape[0]
    me = lax.axis_index("dp")
    mt = lax.axis_index("tp")
    width = queries.shape[1]
    colw = out_weight.shape[1]
    nq = width // HD
    own = reqs // tp
    order = jnp.arange(reqs, dtype=jnp.int32)
    match = slot_request[None, :] == order[:, None]
    slot_of = jnp.sum(jnp.where(match, order[None, :], 0), axis=1).astype(jnp.int32)
    own_request = lax.dynamic_slice_in_dim(slot_request, me, 1, 0)
    own_tip = jnp.sum(jnp.where(order == own_request, accepted_tip, 0)).astype(jnp.int32).reshape(1)
    row_dtype = BF16 if nq % 16 == 0 else F32
    attended, tips, accepted_kv = attend(
        queries, new_kv, cache, cache_len, tree_parent, own_tip, row_dtype
    )
    target = (slot_of[None, :] * nq + jnp.arange(nq, dtype=jnp.int32)[:, None]).reshape(nq * reqs, 1)
    smat = (target == jnp.arange(nq * reqs, dtype=jnp.int32)[None, :]).astype(BF16)
    own_rows = jnp.arange(own, dtype=jnp.int32) * TREE + lax.dynamic_slice_in_dim(
        accepted_tip, mt * own, own, 0
    )
    tip_resid = residual[own_rows].astype(F32)
    resid_tip = lax.dynamic_update_slice_in_dim(jnp.zeros((reqs, colw), F32), tip_resid, mt * own, 0)
    gain = final_gain.astype(F32).reshape(dp, 1, colw)
    hidden, logits = run_main(
        tp, dp, slot_of, tips, smat, resid_tip, gain, attended, out_weight,
        medusa_up, medusa_vocab, residual.reshape(own, TREE, colw),
    )
    return hidden.reshape(own * TREE, colw), logits, accepted_kv


def solution(mesh):
    return jax.shard_map(
        functools.partial(on_device, mesh.shape["tp"], mesh.shape["dp"]),
        mesh=mesh,
        in_specs=(
            P("tp", "dp"),
            P("dp", "tp"),
            P("dp", "tp"),
            P("dp", None, "tp"),
            P("dp"),
            P("dp", None),
            P(),
            P(),
            P("tp", "dp"),
            P(),
            P(None, "dp", "tp"),
            P(None, "tp", "dp"),
        ),
        out_specs=(P("tp", "dp"), P(None, "tp", "dp"), P("dp", None, "tp")),
        check_vma=False,
    )
```

```python
import functools
import math

import jax
import jax.numpy as jnp
from jax import lax
from jax.experimental import pallas as pl
from jax.experimental.pallas import tpu as pltpu
from jax.sharding import PartitionSpec as P

HD = 128
TREE = 48
DEPTH = 5
NEG = -1e30
F32 = jnp.float32
BF16 = jnp.bfloat16
MIB = 1 << 20


def dot(a, b):
    return jnp.dot(a, b, preferred_element_type=F32)


def attend_kernel(
    len_ref, tips_ref, req_ref, par_smem, par_ref, q_ref, new_ref, cache_ref,
    att_ref, row_ref, acc_ref, slot_ref,
):
    group = q_ref.shape[1] // HD
    rows = group * TREE
    length = cache_ref.shape[1]
    scale = 1.0 / math.sqrt(HD)
    live = len_ref[0]
    tip = tips_ref[req_ref[lax.axis_index("dp")]]

    @pl.when(pl.program_id(0) == 0)
    def _():
        for s in range(req_ref.shape[0]):
            slot_ref[req_ref[s]] = s

    nodes = lax.broadcasted_iota(jnp.int32, (TREE, TREE), 1)
    own = lax.broadcasted_iota(jnp.int32, (TREE, TREE), 0)
    step = (par_ref[...] == own).astype(F32).astype(BF16)
    reach = (own == nodes).astype(F32)
    total_reach = reach
    for _ in range(DEPTH - 1):
        reach = lax.dot_general(
            step, reach.astype(BF16), (((0,), (0,)), ((), ())), preferred_element_type=F32
        )
        total_reach = total_reach + reach
    allowed = jnp.concatenate([total_reach] * group, axis=0) > 0.5

    q = jnp.concatenate([q_ref[:, r * HD:(r + 1) * HD] for r in range(group)], axis=0)
    keys = cache_ref[0, :, :HD]
    values = cache_ref[0, :, HD:]
    new_keys = new_ref[:, :HD]
    new_values = new_ref[:, HD:]
    contract = (((1,), (1,)), ((), ()))
    scores = lax.dot_general(q, keys, contract, preferred_element_type=F32) * scale
    place = lax.broadcasted_iota(jnp.int32, (1, length), 1)
    scores = jnp.where(place < live, scores, NEG)
    fresh = lax.dot_general(q, new_keys, contract, preferred_element_type=F32) * scale
    fresh = jnp.where(allowed, fresh, NEG)
    high = jnp.maximum(jnp.max(scores, axis=1, keepdims=True), jnp.max(fresh, axis=1, keepdims=True))
    weights = jnp.exp(scores - high)
    fresh_weights = jnp.exp(fresh - high)
    total = jnp.sum(weights, axis=1, keepdims=True) + jnp.sum(fresh_weights, axis=1, keepdims=True)
    mixed = dot(weights.astype(BF16), values) + dot(fresh_weights.astype(BF16), new_values)
    attended = (mixed / total).astype(BF16)
    for r in range(group):
        att_ref[:, r * HD:(r + 1) * HD] = attended[r * TREE:(r + 1) * TREE]
    lane = lax.broadcasted_iota(jnp.int32, (group, rows), 1)
    want = lax.broadcasted_iota(jnp.int32, (group, rows), 0) * TREE + tip
    row_ref[...] = dot((lane == want).astype(F32).astype(BF16), attended).astype(row_ref.dtype)

    chain = [tip]
    for _ in range(DEPTH - 1):
        last = chain[-1]
        chain.append(jnp.where(last >= 0, par_smem[0, jnp.maximum(last, 0)], -1))
    count = sum((c >= 0).astype(jnp.int32) for c in chain)
    slot = lax.broadcasted_iota(jnp.int32, (16, TREE), 0)
    node = lax.broadcasted_iota(jnp.int32, (16, TREE), 1)
    pick = jnp.zeros((16, TREE), F32)
    for k in range(DEPTH):
        hit = (slot == count - 1 - k) & (node == chain[k])
        pick = pick + hit.astype(F32)
    picked = dot(pick.astype(BF16), new_ref[...])
    acc_ref[0] = picked[:DEPTH].astype(BF16)


def attend(queries, new_kv, cache, cache_len, tree_parent, accepted_tip, slot_request, row_dtype):
    heads = cache.shape[2] // (2 * HD)
    group = queries.shape[1] // (heads * HD)
    length = cache.shape[1]
    smem = pl.BlockSpec(memory_space=pltpu.SMEM)
    return pl.pallas_call(
        attend_kernel,
        grid=(heads,),
        in_specs=[
            smem,
            smem,
            smem,
            smem,
            pl.BlockSpec((1, TREE), lambda g: (0, 0)),
            pl.BlockSpec((TREE, group * HD), lambda g: (0, g)),
            pl.BlockSpec((TREE, 2 * HD), lambda g: (0, g)),
            pl.BlockSpec((1, length, 2 * HD), lambda g: (0, 0, g)),
        ],
        out_specs=[
            pl.BlockSpec((TREE, group * HD), lambda g: (0, g)),
            pl.BlockSpec((group, HD), lambda g: (g, 0)),
            pl.BlockSpec((1, DEPTH, 2 * HD), lambda g: (0, 0, g)),
            smem,
        ],
        out_shape=[
            jax.ShapeDtypeStruct((TREE, heads * group * HD), BF16),
            jax.ShapeDtypeStruct((heads * group, HD), row_dtype),
            jax.ShapeDtypeStruct((1, DEPTH, heads * 2 * HD), BF16),
            jax.ShapeDtypeStruct(slot_request.shape, jnp.int32),
        ],
        compiler_params=pltpu.CompilerParams(vmem_limit_bytes=60 * MIB),
    )(cache_len, accepted_tip, slot_request, tree_parent, tree_parent, queries, new_kv, cache)


def remote(src, dst, send, recv, **where):
    return pltpu.make_async_remote_copy(
        src_ref=src,
        dst_ref=dst,
        send_sem=send,
        recv_sem=recv,
        device_id=where,
        device_id_type=pl.DeviceIdType.MESH,
    )


class Gather:
    def __init__(self, buf, send, recv, me, outer, mid, cond=None):
        self.cond, self.conditional, self.maybe = cond, 0, []
        self.buf, self.send, self.recv = buf, send, recv
        self.outer, self.mid, self.me = outer, mid, me
        self.c = me % 2
        self.m = (me // 2) % mid
        self.o = me // (2 * mid)
        self.started = []

    def at(self, o, m, c):
        return (o * self.mid + m) * 2 + c

    def push(self, block, peer):
        copy = remote(
            self.buf.at[block],
            self.buf.at[block],
            self.send.at[len(self.started)],
            self.recv.at[block],
            dp=peer,
        )
        copy.start()
        self.started.append(copy)

    def arrived(self, block):
        remote(self.buf.at[block], self.buf.at[block], self.send.at[0], self.recv.at[block], dp=self.me).wait_recv()

    def mids(self):
        return [(self.m + d) % self.mid for d in range(1, self.mid)]

    def begin(self):
        for m in self.mids():
            self.push(self.me, self.at(self.o, m, self.c))
        for d in range(1, self.outer):
            self.push(self.me, self.at((self.o + d) % self.outer, self.m, self.c))
        self.push(self.me, self.at(self.o, self.m, 1 - self.c))

    def forward_outer(self, d):
        block = self.at((self.o + d) % self.outer, self.m, self.c)
        self.arrived(block)
        for m in self.mids():
            self.push(block, self.at(self.o, m, self.c))
        self.push(block, self.at(self.o, self.m, 1 - self.c))

    def begin_chain(self):
        for m in self.mids():
            self.push(self.me, self.at(self.o, m, self.c))
        for sign in (-1, 1):
            self.chain_to(sign, self.o)
        self.push(self.me, self.at(self.o, self.m, 1 - self.c))

    def chain_to(self, sign, source, extra=None):
        there = self.o + sign
        where = (there >= 0) & (there < self.outer)
        if extra is not None:
            where = where & extra
        peer = self.at(jnp.clip(there, 0, self.outer - 1), self.m, self.c)
        self.push_when(where, self.at(jnp.clip(source, 0, self.outer - 1), self.m, self.c), peer)

    def push_when(self, where, block, peer):
        index = self.conditional
        self.conditional += 1
        copy = remote(self.buf.at[block], self.buf.at[block], self.cond.at[index], self.recv.at[block], dp=peer)
        pl.when(where)(copy.start)
        self.maybe.append((where, copy))

    def step_chain(self, s):
        for sign in (-1, 1):
            source = self.o + sign * s
            there = (source >= 0) & (source < self.outer)
            block = self.at(jnp.clip(source, 0, self.outer - 1), self.m, self.c)

            @pl.when(there)
            def _(block=block):
                self.arrived(block)

            for m in self.mids():
                self.push_when(there, block, self.at(self.o, m, self.c))
            if s < self.outer - 1:
                self.chain_to(-sign, source, there)
            self.push_when(there, block, self.at(self.o, self.m, 1 - self.c))

    def forward_mid(self):
        for d in range(self.outer):
            for m in self.mids():
                block = self.at((self.o + d) % self.outer, m, self.c)
                self.arrived(block)
                self.push(block, self.at(self.o, self.m, 1 - self.c))

    def finish(self):
        for o in range(self.outer):
            for m in range(self.mid):
                self.arrived(self.at(o, m, 1 - self.c))

    def drain(self):
        for copy in self.started:
            copy.wait_send()
        for where, copy in self.maybe:
            pl.when(where)(copy.wait_send)


def main_kernel(
    tp, dp, outer, mid,
    slot_of, tip_at, slot_req, tips_ref, gain_ref, att_hbm, w_hbm, up_hbm, voc_hbm, resid_hbm,
    hid_out, log_out,
    tipg, w_buf, up_buf, voc_buf, gath, proj, psend, precv, resid_buf,
    xsend, xrecv, hid, part, rec1, acc1, rec2, acc2, rec3, drf, lpart, lrecv,
    w_sem, up_sem, voc_sem, in_sem,
    tip_s, tip_r, x_s, x_r, hid_s, hid_r, c_s, c_r, m_s, m_r, o_s, o_r,
    drf_s, drf_r, bulk_s, bulk_r, bulk_c, l_s, l_r, p_s, p_r,
):
    me = lax.axis_index("dp")
    mt = lax.axis_index("tp")
    c = me % 2
    m = (me // 2) % mid
    o = me // (2 * mid)
    reqs = hid.shape[1]
    heads = up_buf.shape[0]
    width = up_buf.shape[2]
    nq = tips_ref.shape[0]
    colw = hid.shape[2]
    chunk = part.shape[-1]
    row_groups = reqs // 16
    slots = voc_buf.shape[0]
    own_reqs = reqs // tp

    w_copy = pltpu.make_async_copy(w_hbm, w_buf, w_sem)
    w_copy.start()
    own_copy = pltpu.make_async_copy(att_hbm, gath.at[me], in_sem.at[0])
    own_copy.start()
    up_copies = [pltpu.make_async_copy(up_hbm.at[k], up_buf.at[k], up_sem.at[k]) for k in range(heads)]
    voc_copies = [
        pltpu.make_async_copy(voc_hbm.at[k], voc_buf.at[k % slots], voc_sem.at[k]) for k in range(heads)
    ]
    resid_copy = pltpu.make_async_copy(resid_hbm, resid_buf, in_sem.at[1])
    resid_copy.start()
    for copy in up_copies:
        copy.start()
    for copy in voc_copies[:slots]:
        copy.start()

    barrier = pltpu.get_barrier_semaphore()
    for d in range(1, dp):
        pl.semaphore_signal(barrier, inc=1, device_id={"dp": (me + d) % dp}, device_id_type=pl.DeviceIdType.MESH)
    for d in range(1, tp):
        pl.semaphore_signal(barrier, inc=1, device_id={"tp": (mt + d) % tp}, device_id_type=pl.DeviceIdType.MESH)
    pl.semaphore_wait(barrier, dp + tp - 2)

    mine = pl.ds(pl.multiple_of(me * nq, nq), nq)
    tip_copies = []
    for d in range(1, dp):
        copy = remote(tips_ref, tipg.at[mine], tip_s.at[d], tip_r.at[me], dp=(me + d) % dp)
        copy.start()
        tip_copies.append(copy)
    tipg[mine] = tips_ref[...]
    bulk = Gather(gath, bulk_s, bulk_r, me, outer, mid, bulk_c)
    own_copy.wait()
    bulk.begin_chain()
    size = nq * reqs
    line = lax.broadcasted_iota(jnp.int32, (1, size), 1)
    request = jnp.zeros((1, size), jnp.int32)
    for s in range(dp):
        request = jnp.where(line // nq == s, slot_req[s], request)
    down = lax.broadcasted_iota(jnp.int32, (size, size), 0)
    across = lax.broadcasted_iota(jnp.int32, (size, size), 1)
    want = (across % nq) * reqs + request
    smat = (down == want).astype(F32).astype(BF16)
    tall = own_reqs * TREE
    row = lax.broadcasted_iota(jnp.int32, (reqs, tall), 0)
    place = jnp.full((reqs, tall), -1, jnp.int32)
    for r in range(own_reqs):
        place = jnp.where(row == mt * own_reqs + r, r * TREE + tip_at[mt * own_reqs + r], place)
    spot = (lax.broadcasted_iota(jnp.int32, (reqs, tall), 1) == place).astype(F32).astype(BF16)
    resid_copy.wait()
    resid_tip = dot(spot, resid_buf[...].reshape(tall, colw))
    for d in range(1, dp):
        src = (me + d) % dp
        there = pl.ds(pl.multiple_of(src * nq, nq), nq)
        remote(tips_ref, tipg.at[there], tip_s.at[0], tip_r.at[src], dp=me).wait_recv()
    picked = dot(smat, tipg[...].astype(BF16)).astype(BF16)
    tip_rows = jnp.concatenate([picked[i * reqs:(i + 1) * reqs] for i in range(nq)], axis=1)
    w_copy.wait()
    xsend[...] = dot(tip_rows, w_buf[...]) + resid_tip
    x_copies = []
    for d in range(1, tp):
        copy = remote(xsend, xrecv.at[mt], x_s.at[d], x_r.at[mt], tp=(mt + d) % tp)
        copy.start()
        x_copies.append(copy)
    xrecv[mt] = xsend[...]
    for d in range(1, tp):
        src = (mt + d) % tp
        remote(xsend, xrecv.at[src], x_s.at[0], x_r.at[src], tp=mt).wait_recv()
    summed = xrecv[0]
    for d in range(1, tp):
        summed = summed + xrecv[d]
    hid[me] = summed.astype(BF16)
    hid_copies = []
    for d in range(1, dp):
        copy = remote(hid.at[me], hid.at[me], hid_s.at[d], hid_r.at[me], dp=(me + d) % dp)
        copy.start()
        hid_copies.append(copy)
    bulk.step_chain(1)
    for d in range(1, dp):
        src = (me + d) % dp
        remote(hid.at[src], hid.at[src], hid_s.at[0], hid_r.at[src], dp=me).wait_recv()
    squares = jnp.zeros((reqs, colw), F32)
    for d in range(dp):
        block = hid[d].astype(F32)
        squares = squares + block * block
    inverse = lax.rsqrt(jnp.sum(squares, axis=1, keepdims=True) * (1.0 / (dp * colw)) + 1e-05)
    normed = (hid[me].astype(F32) * inverse * gain_ref[me]).astype(BF16)

    for k in range(heads):
        up_copies[k].wait()

    def up_head(k, carry):
        for cg in range(4):
            out = dot(normed, up_buf[k, :, cg * chunk:(cg + 1) * chunk]).astype(BF16)
            for rg in range(row_groups):
                e = (k * row_groups + rg) * 4 + cg
                part[e // 2, cg % 2] = out[rg * 16:(rg + 1) * 16]
        return carry

    lax.fori_loop(0, heads, up_head, 0)

    c_copy = remote(part.at[:, 1 - c], rec1, c_s, c_r, dp=(o * mid + m) * 2 + 1 - c)
    c_copy.start()
    bulk.step_chain(2)
    c_copy.wait_recv()
    half = part[:, c].astype(F32) + rec1[...].astype(F32)
    acc1[...] = half.astype(BF16).reshape(acc1.shape)
    m_copies = []
    for d in range(1, mid):
        pm = (m + d) % mid
        copy = remote(acc1.at[:, pm], rec2.at[m], m_s.at[d], m_r.at[m], dp=(o * mid + pm) * 2 + c)
        copy.start()
        m_copies.append(copy)
    for s in range(3, outer):
        bulk.step_chain(s)
    quarter = acc1[:, m].astype(F32)
    for d in range(1, mid):
        pm = (m + d) % mid
        remote(rec2.at[pm], rec2.at[pm], m_s.at[0], m_r.at[pm], dp=me).wait_recv()
        quarter = quarter + rec2[pm].astype(F32)
    acc2[...] = quarter.astype(BF16)
    o_copies = []
    for d in range(1, outer):
        po = (o + d) % outer
        copy = remote(acc2.at[po], rec3.at[o], o_s.at[d], o_r.at[o], dp=(po * mid + m) * 2 + c)
        copy.start()
        o_copies.append(copy)
    lifted = acc2[o].astype(F32)
    for d in range(1, outer):
        po = (o + d) % outer
        remote(rec3.at[po], rec3.at[po], o_s.at[0], o_r.at[po], dp=me).wait_recv()
        lifted = lifted + rec3[po].astype(F32)
    my_cg = me % 4
    my_rg = (me // 4) % row_groups
    per = chunk // colw
    first = mt * (width // colw) + my_cg * per
    rows16 = pl.ds(pl.multiple_of(my_rg * 16, 16), 16)
    square16 = jnp.zeros((16, colw), F32)
    for d in range(dp):
        block = hid[d, rows16].astype(F32)
        square16 = square16 + block * block
    inverse16 = lax.rsqrt(jnp.sum(square16, axis=1, keepdims=True) * (1.0 / (dp * colw)) + 1e-05)
    skip = jnp.concatenate(
        [
            (hid[first + b, rows16].astype(F32) * inverse16 * gain_ref[first + b]).astype(BF16)
            for b in range(per)
        ],
        axis=1,
    )
    drf[me] = (skip.astype(F32) + lifted / (1.0 + jnp.exp(-lifted))).astype(BF16)
    small = Gather(drf, drf_s, drf_r, me, outer, mid)
    small.begin()
    for d in range(1, outer):
        small.forward_outer(d)
    small.forward_mid()
    small.finish()

    bulk.forward_mid()

    l_copies = []
    for k in range(heads):
        voc_copies[k].wait()
        total = None
        for cg in range(4):
            lhs = jnp.concatenate([drf[(k * row_groups + rg) * 4 + cg] for rg in range(row_groups)], axis=0)
            term = dot(lhs, voc_buf[k % slots, cg * chunk:(cg + 1) * chunk, :])
            total = term if total is None else total + term
        lpart[k] = total.reshape(lpart.shape[1:])
        if k + slots < heads:
            voc_copies[k + slots].start()
        for d in range(1, tp):
            pt = (mt + d) % tp
            copy = remote(lpart.at[k, pt], lrecv.at[mt, k], l_s.at[k, d], l_r.at[k, mt], tp=pt)
            copy.start()
            l_copies.append(copy)

    bulk.finish()

    groups = gath.shape[0] // 4

    def project(g, carry):
        block = gath[pl.ds(g * 4, 4)].reshape(4 * TREE, width)
        proj[pl.ds(g * 4, 4)] = dot(block, w_buf[...]).reshape(4, TREE, colw)
        return carry

    lax.fori_loop(0, groups, project, 0)
    p_copies = []
    for d in range(1, tp):
        pt = (mt + d) % tp

        def fill(i, carry, pt=pt, d=d):
            psend[d - 1, i] = proj[slot_of[pt * own_reqs + i]].astype(BF16)
            return carry

        lax.fori_loop(0, own_reqs, fill, 0)
        copy = remote(psend.at[d - 1], precv.at[mt], p_s.at[d], p_r.at[mt], tp=pt)
        copy.start()
        p_copies.append(copy)

    for k in range(heads):
        for d in range(1, tp):
            src = (mt + d) % tp
            remote(lrecv.at[src, k], lrecv.at[src, k], l_s.at[0, 0], l_r.at[k, src], tp=mt).wait_recv()
    for k in range(heads):
        value = lpart[k, mt]
        for d in range(1, tp):
            value = value + lrecv[(mt + d) % tp, k]
        log_out[k] = value.astype(BF16)

    for d in range(1, tp):
        src = (mt + d) % tp
        remote(precv.at[src], precv.at[src], p_s.at[0], p_r.at[src], tp=mt).wait_recv()

    def finish(i, carry):
        value = resid_buf[i].astype(F32) + proj[slot_of[mt * own_reqs + i]]
        for d in range(1, tp):
            value = value + precv[(mt + d) % tp, i].astype(F32)
        hid_out[i] = value.astype(BF16)
        return carry

    lax.fori_loop(0, own_reqs, finish, 0)

    for copy in tip_copies + x_copies + hid_copies + [c_copy] + m_copies + o_copies + l_copies + p_copies:
        copy.wait_send()
    small.drain()
    bulk.drain()


def run_main(tp, dp, slot_of, tip_at, slot_req, tips, gain, attended, out_weight, up, vocab, residual):
    mid = 2 if dp <= 16 else 4
    outer = dp // (2 * mid)
    heads, colw, width = up.shape
    vcols = vocab.shape[2]
    reqs = slot_of.shape[0]
    own = reqs // tp
    nq = tips.shape[0]
    chunk = heads * (reqs // 16) * width // dp
    slots = heads - 1
    vmem = pl.BlockSpec(memory_space=pltpu.VMEM)
    hbm = pl.BlockSpec(memory_space=pl.ANY)
    smem = pl.BlockSpec(memory_space=pltpu.SMEM)
    dma = pltpu.SemaphoreType.DMA
    return pl.pallas_call(
        functools.partial(main_kernel, tp, dp, outer, mid),
        in_specs=[smem, smem, smem, vmem, vmem, hbm, hbm, hbm, hbm, hbm],
        out_specs=[vmem, vmem],
        out_shape=[
            jax.ShapeDtypeStruct((own, TREE, colw), BF16),
            jax.ShapeDtypeStruct((heads, own, vcols), BF16),
        ],
        scratch_shapes=[
            pltpu.VMEM((dp * nq, HD), tips.dtype),
            pltpu.VMEM((width, colw), BF16),
            pltpu.VMEM((heads, colw, width), BF16),
            pltpu.VMEM((slots, width, vcols), BF16),
            pltpu.VMEM((dp, TREE, width), BF16),
            pltpu.VMEM((dp, TREE, colw), F32),
            pltpu.VMEM((tp - 1, own, TREE, colw), BF16),
            pltpu.VMEM((tp, own, TREE, colw), BF16),
            pltpu.VMEM((own, TREE, colw), BF16),
            pltpu.VMEM((reqs, colw), F32),
            pltpu.VMEM((tp, reqs, colw), F32),
            pltpu.VMEM((dp, reqs, colw), BF16),
            pltpu.VMEM((dp // 2, 2, 16, chunk), BF16),
            pltpu.VMEM((dp // 2, 16, chunk), BF16),
            pltpu.VMEM((outer, mid, 16, chunk), BF16),
            pltpu.VMEM((mid, outer, 16, chunk), BF16),
            pltpu.VMEM((outer, 16, chunk), BF16),
            pltpu.VMEM((outer, 16, chunk), BF16),
            pltpu.VMEM((dp, 16, chunk), BF16),
            pltpu.VMEM((heads, tp, own, vcols), F32),
            pltpu.VMEM((tp, heads, own, vcols), F32),
            dma(()), dma((heads,)), dma((heads,)), dma((2,)),
            dma((dp,)), dma((dp,)), dma((tp,)), dma((tp,)), dma((dp,)), dma((dp,)),
            dma(()), dma(()), dma((mid,)), dma((mid,)), dma((outer,)), dma((outer,)),
            dma((dp,)), dma((dp,)), dma((dp,)), dma((dp,)),
            dma((2 + 2 * (outer - 1) * (mid + 1),)), dma((heads, tp)), dma((heads, tp)), dma((tp,)), dma((tp,)),
        ],
        compiler_params=pltpu.CompilerParams(
            collective_id=0, has_side_effects=True, vmem_limit_bytes=60 * MIB
        ),
    )(slot_of, tip_at, slot_req, tips, gain, attended, out_weight, up, vocab, residual)


def on_device(
    tp, dp,
    residual, queries, new_kv, cache, cache_len, tree_parent, accepted_tip, slot_request,
    out_weight, final_gain, medusa_up, medusa_vocab,
):
    reqs = slot_request.shape[0]
    width = queries.shape[1]
    colw = out_weight.shape[1]
    nq = width // HD
    own = reqs // tp
    row_dtype = BF16 if nq % 16 == 0 else F32
    attended, tips, accepted_kv, slot_of = attend(
        queries, new_kv, cache, cache_len, tree_parent, accepted_tip, slot_request, row_dtype
    )
    gain = final_gain.astype(F32).reshape(dp, 1, colw)
    hidden, logits = run_main(
        tp, dp, slot_of, accepted_tip, slot_request, tips, gain, attended, out_weight,
        medusa_up, medusa_vocab, residual.reshape(own, TREE, colw),
    )
    return hidden.reshape(own * TREE, colw), logits, accepted_kv


def solution(mesh):
    return jax.shard_map(
        functools.partial(on_device, mesh.shape["tp"], mesh.shape["dp"]),
        mesh=mesh,
        in_specs=(
            P("tp", "dp"),
            P("dp", "tp"),
            P("dp", "tp"),
            P("dp", None, "tp"),
            P("dp"),
            P("dp", None),
            P(),
            P(),
            P("tp", "dp"),
            P(),
            P(None, "dp", "tp"),
            P(None, "tp", "dp"),
        ),
        out_specs=(P("tp", "dp"), P(None, "tp", "dp"), P("dp", None, "tp")),
        check_vma=False,
    )
```

```python
import functools
import math

import jax
import jax.numpy as jnp
from jax import lax
from jax.experimental import pallas as pl
from jax.experimental.pallas import tpu as pltpu
from jax.sharding import PartitionSpec as P

HD = 128
TREE = 48
DEPTH = 5
NEG = -1e30
F32 = jnp.float32
BF16 = jnp.bfloat16
MIB = 1 << 20


def dot(a, b):
    return jnp.dot(a, b, preferred_element_type=F32)


def attend_kernel(
    len_ref, tips_ref, req_ref, par_smem, par_ref, q_ref, new_ref, cache_ref,
    att_ref, row_ref, acc_ref, slot_ref,
):
    group = q_ref.shape[1] // HD
    rows = group * TREE
    length = cache_ref.shape[1]
    scale = 1.0 / math.sqrt(HD)
    live = len_ref[0]
    tip = tips_ref[req_ref[lax.axis_index("dp")]]

    @pl.when(pl.program_id(0) == 0)
    def _():
        for s in range(req_ref.shape[0]):
            slot_ref[req_ref[s]] = s

    nodes = lax.broadcasted_iota(jnp.int32, (TREE, TREE), 1)
    own = lax.broadcasted_iota(jnp.int32, (TREE, TREE), 0)
    step = (par_ref[...] == own).astype(F32).astype(BF16)
    reach = (own == nodes).astype(F32)
    total_reach = reach
    for _ in range(DEPTH - 1):
        reach = lax.dot_general(
            step, reach.astype(BF16), (((0,), (0,)), ((), ())), preferred_element_type=F32
        )
        total_reach = total_reach + reach
    allowed = jnp.concatenate([total_reach] * group, axis=0) > 0.5

    q = jnp.concatenate([q_ref[:, r * HD:(r + 1) * HD] for r in range(group)], axis=0)
    keys = cache_ref[0, :, :HD]
    values = cache_ref[0, :, HD:]
    new_keys = new_ref[:, :HD]
    new_values = new_ref[:, HD:]
    contract = (((1,), (1,)), ((), ()))
    scores = lax.dot_general(q, keys, contract, preferred_element_type=F32) * scale
    place = lax.broadcasted_iota(jnp.int32, (1, length), 1)
    scores = jnp.where(place < live, scores, NEG)
    fresh = lax.dot_general(q, new_keys, contract, preferred_element_type=F32) * scale
    fresh = jnp.where(allowed, fresh, NEG)
    high = jnp.maximum(jnp.max(scores, axis=1, keepdims=True), jnp.max(fresh, axis=1, keepdims=True))
    weights = jnp.exp(scores - high)
    fresh_weights = jnp.exp(fresh - high)
    total = jnp.sum(weights, axis=1, keepdims=True) + jnp.sum(fresh_weights, axis=1, keepdims=True)
    mixed = dot(weights.astype(BF16), values) + dot(fresh_weights.astype(BF16), new_values)
    attended = (mixed / total).astype(BF16)
    for r in range(group):
        att_ref[:, r * HD:(r + 1) * HD] = attended[r * TREE:(r + 1) * TREE]
    lane = lax.broadcasted_iota(jnp.int32, (group, rows), 1)
    want = lax.broadcasted_iota(jnp.int32, (group, rows), 0) * TREE + tip
    row_ref[...] = dot((lane == want).astype(F32).astype(BF16), attended).astype(row_ref.dtype)

    chain = [tip]
    for _ in range(DEPTH - 1):
        last = chain[-1]
        chain.append(jnp.where(last >= 0, par_smem[0, jnp.maximum(last, 0)], -1))
    count = sum((c >= 0).astype(jnp.int32) for c in chain)
    slot = lax.broadcasted_iota(jnp.int32, (16, TREE), 0)
    node = lax.broadcasted_iota(jnp.int32, (16, TREE), 1)
    pick = jnp.zeros((16, TREE), F32)
    for k in range(DEPTH):
        hit = (slot == count - 1 - k) & (node == chain[k])
        pick = pick + hit.astype(F32)
    picked = dot(pick.astype(BF16), new_ref[...])
    acc_ref[0] = picked[:DEPTH].astype(BF16)


def attend(queries, new_kv, cache, cache_len, tree_parent, accepted_tip, slot_request, row_dtype):
    heads = cache.shape[2] // (2 * HD)
    group = queries.shape[1] // (heads * HD)
    length = cache.shape[1]
    smem = pl.BlockSpec(memory_space=pltpu.SMEM)
    return pl.pallas_call(
        attend_kernel,
        grid=(heads,),
        in_specs=[
            smem,
            smem,
            smem,
            smem,
            pl.BlockSpec((1, TREE), lambda g: (0, 0)),
            pl.BlockSpec((TREE, group * HD), lambda g: (0, g)),
            pl.BlockSpec((TREE, 2 * HD), lambda g: (0, g)),
            pl.BlockSpec((1, length, 2 * HD), lambda g: (0, 0, g)),
        ],
        out_specs=[
            pl.BlockSpec((TREE, group * HD), lambda g: (0, g)),
            pl.BlockSpec((group, HD), lambda g: (g, 0)),
            pl.BlockSpec((1, DEPTH, 2 * HD), lambda g: (0, 0, g)),
            smem,
        ],
        out_shape=[
            jax.ShapeDtypeStruct((TREE, heads * group * HD), BF16),
            jax.ShapeDtypeStruct((heads * group, HD), row_dtype),
            jax.ShapeDtypeStruct((1, DEPTH, heads * 2 * HD), BF16),
            jax.ShapeDtypeStruct(slot_request.shape, jnp.int32),
        ],
        compiler_params=pltpu.CompilerParams(vmem_limit_bytes=60 * MIB),
    )(cache_len, accepted_tip, slot_request, tree_parent, tree_parent, queries, new_kv, cache)


def remote(src, dst, send, recv, **where):
    return pltpu.make_async_remote_copy(
        src_ref=src,
        dst_ref=dst,
        send_sem=send,
        recv_sem=recv,
        device_id=where,
        device_id_type=pl.DeviceIdType.MESH,
    )


class Gather:
    def __init__(self, buf, send, recv, me, outer, mid, cond=None):
        self.cond, self.conditional, self.maybe = cond, 0, []
        self.buf, self.send, self.recv = buf, send, recv
        self.outer, self.mid, self.me = outer, mid, me
        self.c = me % 2
        self.m = (me // 2) % mid
        self.o = me // (2 * mid)
        self.started = []

    def at(self, o, m, c):
        return (o * self.mid + m) * 2 + c

    def push(self, block, peer):
        copy = remote(
            self.buf.at[block],
            self.buf.at[block],
            self.send.at[len(self.started)],
            self.recv.at[block],
            dp=peer,
        )
        copy.start()
        self.started.append(copy)

    def arrived(self, block):
        remote(self.buf.at[block], self.buf.at[block], self.send.at[0], self.recv.at[block], dp=self.me).wait_recv()

    def mids(self):
        return [(self.m + d) % self.mid for d in range(1, self.mid)]

    def begin(self):
        for m in self.mids():
            self.push(self.me, self.at(self.o, m, self.c))
        for d in range(1, self.outer):
            self.push(self.me, self.at((self.o + d) % self.outer, self.m, self.c))
        self.push(self.me, self.at(self.o, self.m, 1 - self.c))

    def forward_outer(self, d):
        block = self.at((self.o + d) % self.outer, self.m, self.c)
        self.arrived(block)
        for m in self.mids():
            self.push(block, self.at(self.o, m, self.c))
        self.push(block, self.at(self.o, self.m, 1 - self.c))

    def begin_chain(self):
        for m in self.mids():
            self.push(self.me, self.at(self.o, m, self.c))
        for sign in (-1, 1):
            self.chain_to(sign, self.o)
        self.push(self.me, self.at(self.o, self.m, 1 - self.c))

    def chain_to(self, sign, source, extra=None):
        there = self.o + sign
        where = (there >= 0) & (there < self.outer)
        if extra is not None:
            where = where & extra
        peer = self.at(jnp.clip(there, 0, self.outer - 1), self.m, self.c)
        self.push_when(where, self.at(jnp.clip(source, 0, self.outer - 1), self.m, self.c), peer)

    def push_when(self, where, block, peer):
        index = self.conditional
        self.conditional += 1
        copy = remote(self.buf.at[block], self.buf.at[block], self.cond.at[index], self.recv.at[block], dp=peer)
        pl.when(where)(copy.start)
        self.maybe.append((where, copy))

    def step_chain(self, s):
        for sign in (-1, 1):
            source = self.o + sign * s
            there = (source >= 0) & (source < self.outer)
            block = self.at(jnp.clip(source, 0, self.outer - 1), self.m, self.c)

            @pl.when(there)
            def _(block=block):
                self.arrived(block)

            for m in self.mids():
                self.push_when(there, block, self.at(self.o, m, self.c))
            if s < self.outer - 1:
                self.chain_to(-sign, source, there)
            self.push_when(there, block, self.at(self.o, self.m, 1 - self.c))

    def forward_mid(self):
        for d in range(self.outer):
            for m in self.mids():
                block = self.at((self.o + d) % self.outer, m, self.c)
                self.arrived(block)
                self.push(block, self.at(self.o, self.m, 1 - self.c))

    def finish(self):
        for o in range(self.outer):
            for m in range(self.mid):
                self.arrived(self.at(o, m, 1 - self.c))

    def drain(self):
        for copy in self.started:
            copy.wait_send()
        for where, copy in self.maybe:
            pl.when(where)(copy.wait_send)


def main_kernel(
    tp, dp, outer, mid,
    slot_of, tip_at, slot_req, tips_ref, gain_ref, att_hbm, w_hbm, up_hbm, voc_hbm, resid_hbm,
    hid_out, log_out,
    tipg, w_buf, up_buf, voc_buf, gath, proj, psend, precv, resid_buf,
    xsend, xrecv, hid, ssq, part, rec1, acc1, rec2, acc2, rec3, drf, lpart, lrecv,
    w_sem, up_sem, voc_sem, in_sem,
    tip_s, tip_r, x_s, x_r, sq_s, sq_r, hid_s, hid_r, c_s, c_r, m_s, m_r, o_s, o_r,
    drf_s, drf_r, bulk_s, bulk_r, bulk_c, l_s, l_r, p_s, p_r,
):
    me = lax.axis_index("dp")
    mt = lax.axis_index("tp")
    c = me % 2
    m = (me // 2) % mid
    o = me // (2 * mid)
    reqs = hid.shape[1]
    heads = up_buf.shape[0]
    width = up_buf.shape[2]
    nq = tips_ref.shape[0]
    colw = hid.shape[2]
    chunk = part.shape[-1]
    row_groups = reqs // 16
    slots = voc_buf.shape[0]
    own_reqs = reqs // tp

    w_copy = pltpu.make_async_copy(w_hbm, w_buf, w_sem)
    w_copy.start()
    own_copy = pltpu.make_async_copy(att_hbm, gath.at[me], in_sem.at[0])
    own_copy.start()
    up_copies = [pltpu.make_async_copy(up_hbm.at[k], up_buf.at[k], up_sem.at[k]) for k in range(heads)]
    voc_copies = [
        pltpu.make_async_copy(voc_hbm.at[k], voc_buf.at[k % slots], voc_sem.at[k]) for k in range(heads)
    ]
    resid_copy = pltpu.make_async_copy(resid_hbm, resid_buf, in_sem.at[1])
    resid_copy.start()
    for copy in up_copies:
        copy.start()
    for copy in voc_copies[:slots]:
        copy.start()

    barrier = pltpu.get_barrier_semaphore()
    for d in range(1, dp):
        pl.semaphore_signal(barrier, inc=1, device_id={"dp": (me + d) % dp}, device_id_type=pl.DeviceIdType.MESH)
    for d in range(1, tp):
        pl.semaphore_signal(barrier, inc=1, device_id={"tp": (mt + d) % tp}, device_id_type=pl.DeviceIdType.MESH)
    pl.semaphore_wait(barrier, dp + tp - 2)

    mine = pl.ds(pl.multiple_of(me * nq, nq), nq)
    tip_copies = []
    for d in range(1, dp):
        copy = remote(tips_ref, tipg.at[mine], tip_s.at[d], tip_r.at[me], dp=(me + d) % dp)
        copy.start()
        tip_copies.append(copy)
    tipg[mine] = tips_ref[...]
    bulk = Gather(gath, bulk_s, bulk_r, me, outer, mid, bulk_c)
    own_copy.wait()
    bulk.begin_chain()
    size = nq * reqs
    line = lax.broadcasted_iota(jnp.int32, (1, size), 1)
    request = jnp.zeros((1, size), jnp.int32)
    for s in range(dp):
        request = jnp.where(line // nq == s, slot_req[s], request)
    down = lax.broadcasted_iota(jnp.int32, (size, size), 0)
    across = lax.broadcasted_iota(jnp.int32, (size, size), 1)
    want = (across % nq) * reqs + request
    smat = (down == want).astype(F32).astype(BF16)
    tall = own_reqs * TREE
    row = lax.broadcasted_iota(jnp.int32, (reqs, tall), 0)
    place = jnp.full((reqs, tall), -1, jnp.int32)
    for r in range(own_reqs):
        place = jnp.where(row == mt * own_reqs + r, r * TREE + tip_at[mt * own_reqs + r], place)
    spot = (lax.broadcasted_iota(jnp.int32, (reqs, tall), 1) == place).astype(F32).astype(BF16)
    resid_copy.wait()
    resid_tip = dot(spot, resid_buf[...].reshape(tall, colw))
    for d in range(1, dp):
        src = (me + d) % dp
        there = pl.ds(pl.multiple_of(src * nq, nq), nq)
        remote(tips_ref, tipg.at[there], tip_s.at[0], tip_r.at[src], dp=me).wait_recv()
    picked = dot(smat, tipg[...].astype(BF16)).astype(BF16)
    tip_rows = jnp.concatenate([picked[i * reqs:(i + 1) * reqs] for i in range(nq)], axis=1)
    w_copy.wait()
    xsend[...] = dot(tip_rows, w_buf[...]) + resid_tip
    x_copies = []
    for d in range(1, tp):
        copy = remote(xsend, xrecv.at[mt], x_s.at[d], x_r.at[mt], tp=(mt + d) % tp)
        copy.start()
        x_copies.append(copy)
    xrecv[mt] = xsend[...]
    for d in range(1, tp):
        src = (mt + d) % tp
        remote(xsend, xrecv.at[src], x_s.at[0], x_r.at[src], tp=mt).wait_recv()
    summed = xrecv[0]
    for d in range(1, tp):
        summed = summed + xrecv[d]
    hid[me] = summed.astype(BF16)
    mine_sq = hid[me].astype(F32)
    mine_sq = mine_sq * mine_sq
    folded = mine_sq[:, :HD]
    for b in range(1, colw // HD):
        folded = folded + mine_sq[:, b * HD:(b + 1) * HD]
    ssq[me] = folded
    sq_copies = []
    for d in range(1, dp):
        copy = remote(ssq.at[me], ssq.at[me], sq_s.at[d], sq_r.at[me], dp=(me + d) % dp)
        copy.start()
        sq_copies.append(copy)
    hid_copies = []
    for d in range(1, dp):
        copy = remote(hid.at[me], hid.at[me], hid_s.at[d], hid_r.at[me], dp=(me + d) % dp)
        copy.start()
        hid_copies.append(copy)
    bulk.step_chain(1)
    for d in range(1, dp):
        src = (me + d) % dp
        remote(ssq.at[src], ssq.at[src], sq_s.at[0], sq_r.at[src], dp=me).wait_recv()
    squares = ssq[0]
    for d in range(1, dp):
        squares = squares + ssq[d]
    inverse = lax.rsqrt(jnp.sum(squares, axis=1, keepdims=True) * (1.0 / (dp * colw)) + 1e-05)
    normed = (hid[me].astype(F32) * inverse * gain_ref[me]).astype(BF16)

    for k in range(heads):
        up_copies[k].wait()

    def up_head(k, carry):
        for cg in range(4):
            out = dot(normed, up_buf[k, :, cg * chunk:(cg + 1) * chunk]).astype(BF16)
            for rg in range(row_groups):
                e = (k * row_groups + rg) * 4 + cg
                part[e // 2, cg % 2] = out[rg * 16:(rg + 1) * 16]
        return carry

    lax.fori_loop(0, heads, up_head, 0)

    c_copy = remote(part.at[:, 1 - c], rec1, c_s, c_r, dp=(o * mid + m) * 2 + 1 - c)
    c_copy.start()
    bulk.step_chain(2)
    c_copy.wait_recv()
    half = part[:, c].astype(F32) + rec1[...].astype(F32)
    acc1[...] = half.astype(BF16).reshape(acc1.shape)
    m_copies = []
    for d in range(1, mid):
        pm = (m + d) % mid
        copy = remote(acc1.at[:, pm], rec2.at[m], m_s.at[d], m_r.at[m], dp=(o * mid + pm) * 2 + c)
        copy.start()
        m_copies.append(copy)
    for s in range(3, outer):
        bulk.step_chain(s)
    quarter = acc1[:, m].astype(F32)
    for d in range(1, mid):
        pm = (m + d) % mid
        remote(rec2.at[pm], rec2.at[pm], m_s.at[0], m_r.at[pm], dp=me).wait_recv()
        quarter = quarter + rec2[pm].astype(F32)
    acc2[...] = quarter.astype(BF16)
    o_copies = []
    for d in range(1, outer):
        po = (o + d) % outer
        copy = remote(acc2.at[po], rec3.at[o], o_s.at[d], o_r.at[o], dp=(po * mid + m) * 2 + c)
        copy.start()
        o_copies.append(copy)
    lifted = acc2[o].astype(F32)
    for d in range(1, outer):
        po = (o + d) % outer
        remote(rec3.at[po], rec3.at[po], o_s.at[0], o_r.at[po], dp=me).wait_recv()
        lifted = lifted + rec3[po].astype(F32)
    my_cg = me % 4
    my_rg = (me // 4) % row_groups
    per = chunk // colw
    first = mt * (width // colw) + my_cg * per
    rows16 = pl.ds(pl.multiple_of(my_rg * 16, 16), 16)
    square16 = ssq[0, rows16]
    for d in range(1, dp):
        square16 = square16 + ssq[d, rows16]
    for d in range(1, dp):
        src = (me + d) % dp
        remote(hid.at[src], hid.at[src], hid_s.at[0], hid_r.at[src], dp=me).wait_recv()
    inverse16 = lax.rsqrt(jnp.sum(square16, axis=1, keepdims=True) * (1.0 / (dp * colw)) + 1e-05)
    skip = jnp.concatenate(
        [
            (hid[first + b, rows16].astype(F32) * inverse16 * gain_ref[first + b]).astype(BF16)
            for b in range(per)
        ],
        axis=1,
    )
    drf[me] = (skip.astype(F32) + lifted / (1.0 + jnp.exp(-lifted))).astype(BF16)
    bulk.forward_mid()
    small = Gather(drf, drf_s, drf_r, me, outer, mid)
    small.begin()
    for d in range(1, outer):
        small.forward_outer(d)
    small.forward_mid()
    small.finish()

    bulk.finish()

    groups = gath.shape[0] // 4

    def project(g, carry):
        block = gath[pl.ds(g * 4, 4)].reshape(4 * TREE, width)
        proj[pl.ds(g * 4, 4)] = dot(block, w_buf[...]).reshape(4, TREE, colw)
        return carry

    lax.fori_loop(0, groups, project, 0)
    p_copies = []
    for d in range(1, tp):
        pt = (mt + d) % tp

        def fill(i, carry, pt=pt, d=d):
            psend[d - 1, i] = proj[slot_of[pt * own_reqs + i]].astype(BF16)
            return carry

        lax.fori_loop(0, own_reqs, fill, 0)
        copy = remote(psend.at[d - 1], precv.at[mt], p_s.at[d], p_r.at[mt], tp=pt)
        copy.start()
        p_copies.append(copy)

    l_copies = []
    for k in range(heads):
        voc_copies[k].wait()
        total = None
        for cg in range(4):
            lhs = jnp.concatenate([drf[(k * row_groups + rg) * 4 + cg] for rg in range(row_groups)], axis=0)
            term = dot(lhs, voc_buf[k % slots, cg * chunk:(cg + 1) * chunk, :])
            total = term if total is None else total + term
        lpart[k] = total.reshape(lpart.shape[1:])
        if k + slots < heads:
            voc_copies[k + slots].start()
        for d in range(1, tp):
            pt = (mt + d) % tp
            copy = remote(lpart.at[k, pt], lrecv.at[mt, k], l_s.at[k, d], l_r.at[k, mt], tp=pt)
            copy.start()
            l_copies.append(copy)

    for k in range(heads):
        for d in range(1, tp):
            src = (mt + d) % tp
            remote(lrecv.at[src, k], lrecv.at[src, k], l_s.at[0, 0], l_r.at[k, src], tp=mt).wait_recv()
    for k in range(heads):
        value = lpart[k, mt]
        for d in range(1, tp):
            value = value + lrecv[(mt + d) % tp, k]
        log_out[k] = value.astype(BF16)

    for d in range(1, tp):
        src = (mt + d) % tp
        remote(precv.at[src], precv.at[src], p_s.at[0], p_r.at[src], tp=mt).wait_recv()

    def finish(i, carry):
        value = resid_buf[i].astype(F32) + proj[slot_of[mt * own_reqs + i]]
        for d in range(1, tp):
            value = value + precv[(mt + d) % tp, i].astype(F32)
        hid_out[i] = value.astype(BF16)
        return carry

    lax.fori_loop(0, own_reqs, finish, 0)

    for copy in tip_copies + x_copies + sq_copies + hid_copies + [c_copy] + m_copies + o_copies + l_copies + p_copies:
        copy.wait_send()
    small.drain()
    bulk.drain()


def run_main(tp, dp, slot_of, tip_at, slot_req, tips, gain, attended, out_weight, up, vocab, residual):
    mid = 2 if dp <= 16 else 4
    outer = dp // (2 * mid)
    heads, colw, width = up.shape
    vcols = vocab.shape[2]
    reqs = slot_of.shape[0]
    own = reqs // tp
    nq = tips.shape[0]
    chunk = heads * (reqs // 16) * width // dp
    slots = heads - 1
    vmem = pl.BlockSpec(memory_space=pltpu.VMEM)
    hbm = pl.BlockSpec(memory_space=pl.ANY)
    smem = pl.BlockSpec(memory_space=pltpu.SMEM)
    dma = pltpu.SemaphoreType.DMA
    return pl.pallas_call(
        functools.partial(main_kernel, tp, dp, outer, mid),
        in_specs=[smem, smem, smem, vmem, vmem, hbm, hbm, hbm, hbm, hbm],
        out_specs=[vmem, vmem],
        out_shape=[
            jax.ShapeDtypeStruct((own, TREE, colw), BF16),
            jax.ShapeDtypeStruct((heads, own, vcols), BF16),
        ],
        scratch_shapes=[
            pltpu.VMEM((dp * nq, HD), tips.dtype),
            pltpu.VMEM((width, colw), BF16),
            pltpu.VMEM((heads, colw, width), BF16),
            pltpu.VMEM((slots, width, vcols), BF16),
            pltpu.VMEM((dp, TREE, width), BF16),
            pltpu.VMEM((dp, TREE, colw), F32),
            pltpu.VMEM((tp - 1, own, TREE, colw), BF16),
            pltpu.VMEM((tp, own, TREE, colw), BF16),
            pltpu.VMEM((own, TREE, colw), BF16),
            pltpu.VMEM((reqs, colw), F32),
            pltpu.VMEM((tp, reqs, colw), F32),
            pltpu.VMEM((dp, reqs, colw), BF16),
            pltpu.VMEM((dp, reqs, HD), F32),
            pltpu.VMEM((dp // 2, 2, 16, chunk), BF16),
            pltpu.VMEM((dp // 2, 16, chunk), BF16),
            pltpu.VMEM((outer, mid, 16, chunk), BF16),
            pltpu.VMEM((mid, outer, 16, chunk), BF16),
            pltpu.VMEM((outer, 16, chunk), BF16),
            pltpu.VMEM((outer, 16, chunk), BF16),
            pltpu.VMEM((dp, 16, chunk), BF16),
            pltpu.VMEM((heads, tp, own, vcols), F32),
            pltpu.VMEM((tp, heads, own, vcols), F32),
            dma(()), dma((heads,)), dma((heads,)), dma((2,)),
            dma((dp,)), dma((dp,)), dma((tp,)), dma((tp,)), dma((dp,)), dma((dp,)), dma((dp,)), dma((dp,)),
            dma(()), dma(()), dma((mid,)), dma((mid,)), dma((outer,)), dma((outer,)),
            dma((dp,)), dma((dp,)), dma((dp,)), dma((dp,)),
            dma((2 + 2 * (outer - 1) * (mid + 1),)), dma((heads, tp)), dma((heads, tp)), dma((tp,)), dma((tp,)),
        ],
        compiler_params=pltpu.CompilerParams(
            collective_id=0, has_side_effects=True, vmem_limit_bytes=60 * MIB
        ),
    )(slot_of, tip_at, slot_req, tips, gain, attended, out_weight, up, vocab, residual)


def on_device(
    tp, dp,
    residual, queries, new_kv, cache, cache_len, tree_parent, accepted_tip, slot_request,
    out_weight, final_gain, medusa_up, medusa_vocab,
):
    reqs = slot_request.shape[0]
    width = queries.shape[1]
    colw = out_weight.shape[1]
    nq = width // HD
    own = reqs // tp
    row_dtype = BF16 if nq % 16 == 0 else F32
    attended, tips, accepted_kv, slot_of = attend(
        queries, new_kv, cache, cache_len, tree_parent, accepted_tip, slot_request, row_dtype
    )
    gain = final_gain.astype(F32).reshape(dp, 1, colw)
    hidden, logits = run_main(
        tp, dp, slot_of, accepted_tip, slot_request, tips, gain, attended, out_weight,
        medusa_up, medusa_vocab, residual.reshape(own, TREE, colw),
    )
    return hidden.reshape(own * TREE, colw), logits, accepted_kv


def solution(mesh):
    return jax.shard_map(
        functools.partial(on_device, mesh.shape["tp"], mesh.shape["dp"]),
        mesh=mesh,
        in_specs=(
            P("tp", "dp"),
            P("dp", "tp"),
            P("dp", "tp"),
            P("dp", None, "tp"),
            P("dp"),
            P("dp", None),
            P(),
            P(),
            P("tp", "dp"),
            P(),
            P(None, "dp", "tp"),
            P(None, "tp", "dp"),
        ),
        out_specs=(P("tp", "dp"), P(None, "tp", "dp"), P("dp", None, "tp")),
        check_vma=False,
    )
```
